32 devices in a mesh: wide: 16 (over z, x, core), depth: 2 (over y).
Axes of the slice: x: 2, y: 2, z: 4, core: 2. Of those that a mesh axis runs over, the one named last changes fastest.
Arguments:
- schur: float32 [16, 2, 1536, 1536], P('wide', 'depth'), as said below
- loads: float32 [16, 2, 1536, 128], P('wide', 'depth'), may hold values from -6 to 6
- face_sizes: int32 [16, 2, 6], P('wide', 'depth'), may hold values from 64 to 256, as said below
- face_dir: int32 [16, 2, 6], P('wide', 'depth'), may hold values from 0 to 5, as said below
Outputs:
- displacement: float32 [16, 2, 1536, 128], P('wide', 'depth')
- residual: float32 [16, 2, 1536, 128], P('wide', 'depth')
The draws below stay inside these ranges and needn't reach their ends.
Inputs may be any that keep to these rules, and one draw needn't show every extreme that they name: `face_sizes`: A face slot and the neighbour's slot facing back across the same face have the same size; some slot holds 256 used unknowns and some holds 64. `face_dir`: each subdomain's six entries are 0 to 5 in some order: 0 faces the lower neighbour along wide, 1 the upper one, 2 the lower neighbour along depth, 3 the upper one, 4 and 5 the supported top and bottom surfaces. `schur`: each subdomain's matrix is symmetric and positive definite.
All inputs are finite; a program needn't handle non-finite values.
Results may differ from the reference program's by a relative error of at most 0.00017.
Values sent between devices are 32-bit elements; how exact they have to be, the bound alone decides.
No kernel may reach another device: no remote copies, remote signals or barrier semaphores. Data moves between devices by JAX's collectives and lax.ppermute only.
A program may use at most 128 MiB of HBM per device.

```python
import jax
import jax.numpy as jnp
from jax import lax

FCAP = 256
NRHS = 128
ITERS = 2
M = 1536
GRID_W = 16
GRID_D = 2


def face_tables(key):
    first, second = jax.random.split(jax.random.fold_in(key, 7))
    base = jax.random.randint(first, (GRID_W, GRID_D, 6), FCAP // 4, FCAP + 1).astype(jnp.int32)
    base = base.at[0, 0, 4].set(FCAP).at[0, 0, 5].set(FCAP // 4)
    lower_w = jnp.concatenate([base[:1, :, 0], base[:-1, :, 1]], axis=0)
    lower_d = jnp.concatenate([base[:, :1, 2], base[:, :-1, 3]], axis=1)
    sized = jnp.stack([lower_w, base[..., 1], lower_d, base[..., 3], base[..., 4], base[..., 5]], axis=-1)
    scores = jax.random.randint(second, (GRID_W, GRID_D, 6), 0, 1000).astype(jnp.int32) * 6 + jnp.arange(6, dtype=jnp.int32)
    order = jnp.argsort(scores, axis=-1).astype(jnp.int32)
    slot_sizes = jnp.take_along_axis(sized, order, axis=-1).astype(jnp.int32)
    return (slot_sizes, order)


def draw_face_sizes(key, part):
    return face_tables(key)[0]


def draw_face_dir(key, part):
    return face_tables(key)[1]


def draw_schur(key, part):
    first, second, third = jax.random.split(jax.random.fold_in(key, 11), 3)
    noise = jax.random.normal(first, (GRID_W, GRID_D, M, M), jnp.float32)
    sym = (noise + jnp.swapaxes(noise, -1, -2)) * (0.5 / jnp.sqrt(2.0 * M))
    diag = jax.random.uniform(second, (GRID_W, GRID_D, M), jnp.float32, 1.5, 3.0)
    places = jnp.arange(FCAP, dtype=jnp.float32)
    kernel = jnp.exp(-jnp.abs(places[:, None] - places[None, :]) / (FCAP / 4.0))
    banded = (jnp.eye(6, dtype=jnp.float32)[:, None, :, None] * kernel[None, :, None, :]).reshape(M, M)
    amplitude = jax.random.uniform(third, (GRID_W, GRID_D, 6), jnp.float32, 0.06, 0.14)
    rooted = jnp.repeat(jnp.sqrt(amplitude), FCAP, axis=-1)
    smooth = rooted[..., :, None] * banded * rooted[..., None, :]
    return sym + diag[..., None] * jnp.eye(M, dtype=jnp.float32) + smooth


def level_of(own_key, dims, cuts, low, largest):
    def one(dim, blocks):
        heights = jax.random.uniform(jax.random.fold_in(jax.random.fold_in(own_key, 6), dim), (blocks,), jnp.float32, low / len(cuts), largest / len(cuts))
        return jnp.repeat(jnp.exp(heights), dims[dim] // blocks).reshape((-1,) + (1,) * (len(dims) - dim - 1))

    loudness = one(*cuts[0])
    for cut in cuts[1:]:
        loudness = loudness * one(*cut)
    return loudness


def scatter_about(own_key, shape, spread, most, cuts=(), kind=jnp.bfloat16):
    result = spread * jax.random.normal(own_key, shape, jnp.float32)
    if cuts:
        result = result * level_of(own_key, shape, cuts, -0.22, 0.18)
    return jnp.clip(result, -most, most).astype(kind)


def setup_inputs(seed: int = 0) -> dict:
    streams_of = jax.random.split(jax.random.key(seed), 5)
    return {
        "schur": draw_schur(jax.random.fold_in(streams_of[4], 71), 0),
        "loads": scatter_about(streams_of[1], (GRID_W, GRID_D, M, NRHS), 1.0, 6.0, ((0, 16), (1, 2)), jnp.float32),
        "face_sizes": draw_face_sizes(jax.random.fold_in(streams_of[4], 71), 0),
        "face_dir": draw_face_dir(jax.random.fold_in(streams_of[4], 71), 0),
    }


OMEGA = 0.6

def to_dirs(select, x):
    return jnp.einsum('...kd,...kfr->...dfr', select, x, precision=lax.Precision.HIGHEST)

def to_slots(select, x):
    return jnp.einsum('...kd,...dfr->...kfr', select, x, precision=lax.Precision.HIGHEST)

def assemble(select, parts):
    facing = to_dirs(select, parts)
    blank_w = jnp.zeros_like(facing[:1, :, 0])
    blank_d = jnp.zeros_like(facing[:, :1, 0])
    from_lower_w = jnp.concatenate([blank_w, facing[:-1, :, 1]], axis=0)
    from_upper_w = jnp.concatenate([facing[1:, :, 0], blank_w], axis=0)
    from_lower_d = jnp.concatenate([blank_d, facing[:, :-1, 3]], axis=1)
    from_upper_d = jnp.concatenate([facing[:, 1:, 2], blank_d], axis=1)
    blank = jnp.zeros_like(facing[:, :, 0])
    arrived = jnp.stack([from_lower_w, from_upper_w, from_lower_d, from_upper_d, blank, blank], axis=2)
    return parts + to_slots(select, arrived)

def reference(schur, loads, face_sizes, face_dir):
    slot_rows = FCAP
    cases = loads.shape[-1]
    mask = (jnp.arange(slot_rows, dtype=jnp.int32)[None, None, None, :] < face_sizes[..., None]).astype(jnp.float32)
    select = (face_dir[..., :, None] == jnp.arange(6, dtype=jnp.int32)).astype(jnp.float32)
    shaped = schur.reshape(GRID_W, GRID_D, 6, slot_rows, 6, slot_rows)
    blocks = jnp.stack([shaped[:, :, k, :, k, :] for k in range(6)], axis=2)
    summed = assemble(select, blocks)
    ident = jnp.eye(slot_rows, dtype=jnp.float32)
    summed = summed * mask[..., :, None] * mask[..., None, :] + ident * (1.0 - mask[..., :, None])
    factor = jnp.linalg.cholesky(summed)
    inverse = jax.scipy.linalg.cho_solve((factor, True), jnp.broadcast_to(ident, summed.shape))
    flat_schur = schur.reshape(GRID_W * GRID_D, M, M)

    def partial_value(disp):
        flat = disp.reshape(GRID_W * GRID_D, M, cases)
        applied = lax.map(lambda pair: jnp.dot(pair[0], pair[1], precision=lax.Precision.HIGHEST), (flat_schur, flat))
        local = loads - applied.reshape(GRID_W, GRID_D, M, cases)
        return local.reshape(GRID_W, GRID_D, 6, slot_rows, cases) * mask[..., None]
    disp = jnp.zeros((GRID_W, GRID_D, 6, slot_rows, cases), jnp.float32)
    for step in range(ITERS):
        resid = assemble(select, partial_value(disp))
        update = jnp.einsum('...fg,...gc->...fc', inverse, resid, precision=lax.Precision.HIGHEST)
        disp = disp + OMEGA * update
    final = assemble(select, partial_value(disp))
    return (disp.reshape(GRID_W, GRID_D, M, cases), final.reshape(GRID_W, GRID_D, M, cases))
```

```python
import functools

import jax
import jax.numpy as jnp
from jax import lax
from jax.experimental import pallas as pl
from jax.experimental.pallas import tpu as pltpu
from jax.sharding import PartitionSpec as P

ITERS = 2
OMEGA = 0.6

SLOTS = 6
LANES = 128
OUTER = 64
MICRO = 8
F32 = jnp.float32
BF16 = jnp.bfloat16
SMEM = pl.BlockSpec(memory_space=pltpu.SMEM)
VMEM = pl.BlockSpec(memory_space=pltpu.VMEM)
HBM = pl.BlockSpec(memory_space=pltpu.HBM)


def role_list(mesh):
    return [(axis, turn) for axis in ("wide", "depth") for turn in (0, 1) if mesh.shape[axis] > 1 + turn]


def role_slot(mesh, dirs_ref, role):
    axis, turn = role
    index = lax.axis_index(axis)
    count = mesh.shape[axis]
    upper = (index + turn) % 2 == 0
    facing = jnp.where(upper, 1, 0) + (0 if axis == "wide" else 2)
    slot = jnp.int32(0)
    for k in range(SLOTS):
        slot = slot + jnp.where(dirs_ref[k] == facing, k, 0)
    there = jnp.where(upper, index + 1 < count, index > 0)
    return slot, there


def exchange(mesh, role, value):
    axis, turn = role
    other = "depth" if axis == "wide" else "wide"
    count, rest = mesh.shape[axis], mesh.shape[other]
    pairs, left = [], []
    for line in range(rest):
        met = set()
        for low in range(turn, count - 1, 2):
            pairs.append(((low, line), (low + 1, line)))
            met |= {low, low + 1}
        left.append([(i, line) for i in range(count) if i not in met])
    alone = [spot for spots in left for spot in spots]
    pairs += list(zip(alone[::2], alone[1::2]))

    def flat(spot):
        place = {axis: spot[0], other: spot[1]}
        return place["wide"] * mesh.shape["depth"] + place["depth"]

    perm = []
    for one, two in pairs:
        perm += [(flat(one), flat(two)), (flat(two), flat(one))]
    return lax.ppermute(value, ("wide", "depth"), sorted(perm))


def spread_row(x, k):
    return jnp.broadcast_to(x[k : k + 1, :], x.shape)


def tree_sum(terms):
    while len(terms) > 1:
        terms = [terms[i] + terms[i + 1] if i + 1 < len(terms) else terms[i] for i in range(0, len(terms), 2)]
    return terms[0]


def invert_diagonal(d):
    rows, packs = len(d), len(d[0])
    lane = lax.broadcasted_iota(jnp.int32, (MICRO, LANES), 1)
    sub = lax.broadcasted_iota(jnp.int32, (MICRO, LANES), 0)
    half = lane & OUTER
    local = lane & (OUTER - 1)
    for q in range(rows):
        own = (local >= q * MICRO) & (local < (q + 1) * MICRO)
        spots = [half + (q * MICRO + j) for j in range(MICRO)]
        cols = [[jnp.take_along_axis(d[q][p], spots[j], axis=1) for j in range(MICRO)] for p in range(packs)]
        scales = [[None] * MICRO for _ in range(packs)]
        for k in range(MICRO):
            pivot_row = sub == k
            for p in range(packs):
                c = cols[p]
                scale = 1.0 / spread_row(c[k], k)
                scales[p][k] = scale
                h = jnp.where(pivot_row, 0.0, c[k]) * scale
                for j in range(MICRO):
                    if j != k:
                        c[j] = c[j] - h * spread_row(c[j], k)
                c[k] = jnp.where(pivot_row, 1.0, -h)
        for p in range(packs):
            scale = scales[p][0]
            for k in range(1, MICRO):
                scale = jnp.where(sub == k, scales[p][k], scale)
            row = jnp.where(own, jnp.where(local == sub + q * MICRO, 1.0, 0.0), d[q][p])
            row = tree_sum([cols[p][j] * spread_row(row, j) for j in range(MICRO)]) * scale
            spread = [spread_row(row, j) for j in range(MICRO)]
            for step in range(1, rows):
                i = (q + step) % rows
                x = d[i][p]
                change = tree_sum([jnp.take_along_axis(x, spots[j], axis=1) * spread[j] for j in range(MICRO)])
                d[i][p] = jnp.where(own, 0.0, x) - change
            d[q][p] = row
    return d


def split(x):
    high = x.astype(BF16)
    return high, (x - high.astype(F32)).astype(BF16)


def invert_blocks(a_ref):
    count, size = a_ref.shape[0], a_ref.shape[-1]
    lane = lax.broadcasted_iota(jnp.int32, (MICRO, LANES), 1)
    for block in range(size // OUTER):
        r0 = block * OUTER
        tile, h = divmod(r0, LANES)
        h //= OUTER
        tl = slice(tile * LANES, (tile + 1) * LANES)
        d = []
        for i in range(OUTER // MICRO):
            rows = slice(r0 + i * MICRO, r0 + (i + 1) * MICRO)
            line = []
            for p in range(count // 2):
                x, y = a_ref[2 * p, rows, tl], a_ref[2 * p + 1, rows, tl]
                if h == 0:
                    line.append(jnp.where(lane < OUTER, x, pltpu.roll(y, OUTER, 1)))
                else:
                    line.append(jnp.where(lane < OUTER, pltpu.roll(x, OUTER, 1), y))
            d.append(line)
        d = invert_diagonal(d)
        lane_row = lax.broadcasted_iota(jnp.int32, (OUTER, LANES), 1)
        own_row = (lane_row >= OUTER * h) & (lane_row < OUTER * (h + 1))
        lane_all = lax.broadcasted_iota(jnp.int32, (size, LANES), 1)
        own_all = (lane_all >= OUTER * h) & (lane_all < OUTER * (h + 1))
        for g in range(count):
            p, s = divmod(g, 2)
            w = jnp.concatenate([d[i][p] for i in range(OUTER // MICRO)], 0)
            if s != h:
                w = pltpu.roll(w, OUTER, 1)
            w = jnp.where(own_row, w, 0.0)
            w_high = w.astype(BF16)
            w_mixed = (w + pltpu.roll(w - w_high.astype(F32), OUTER, 1)).astype(BF16)
            high, low = split(a_ref[g, r0 : r0 + OUTER, :])
            zero = jnp.zeros_like(low)
            right = jnp.concatenate([high, high, low, zero] if h == 0 else [high, high, zero, low], 0)
            row = jnp.dot(jnp.concatenate([w_mixed, w_high], 1), right, preferred_element_type=F32)
            row = jnp.concatenate(
                [
                    jnp.where(own_row, w, row[:, c * LANES : (c + 1) * LANES]) if c == tile else row[:, c * LANES : (c + 1) * LANES]
                    for c in range(size // LANES)
                ],
                1,
            )
            column = a_ref[g, :, tl]
            c_high = column.astype(BF16)
            c_mixed = jnp.where(own_all, column, pltpu.roll(column - c_high.astype(F32), OUTER, 1)).astype(BF16)
            high, low = split(row)
            right = jnp.concatenate([high, high, low, zero] if h == 0 else [high, high, zero, low], 0)
            change = jnp.dot(jnp.concatenate([c_mixed, c_high], 1), right, preferred_element_type=F32)
            for c in range(size // LANES):
                cl = slice(c * LANES, (c + 1) * LANES)
                base = a_ref[g, :, cl]
                if c == tile:
                    base = jnp.where(own_all, 0.0, base)
                a_ref[g, :, cl] = base - change[:, cl]
            a_ref[g, r0 : r0 + OUTER, :] = row


def slot_rows(slot, rows):
    return pl.ds(pl.multiple_of(slot * rows, rows), rows)


def row_mask(rows, size, lanes=LANES):
    return lax.broadcasted_iota(jnp.int32, (rows, lanes), 0) < size


def pack_kernel(mesh, roles, dirs, sizes, matrix, loads, *rest):
    outs, (block, load, sems) = rest[: len(roles)], rest[len(roles) :]
    rows = block.shape[1]
    cases = load.shape[2]
    copies = []
    for n, role in enumerate(roles):
        slot, _ = role_slot(mesh, dirs, role)
        at = slot_rows(slot, rows)
        one = pltpu.make_async_copy(matrix.at[at, at], block.at[n], sems.at[n, 0])
        two = pltpu.make_async_copy(loads.at[at, :], load.at[n], sems.at[n, 1])
        one.start()
        two.start()
        copies.append((one, two, slot))
    for n, (one, two, slot) in enumerate(copies):
        one.wait()
        two.wait()
        outs[n][:, :rows] = block[n]
        outs[n][:, rows:] = jnp.where(row_mask(rows, sizes[slot], cases), load[n], 0.0)


def split_kernel(matrix, high_ref, low_ref, diagonal, buffer, sems):
    order = matrix.shape[0]
    rows = diagonal.shape[1]
    chunk = buffer.shape[1]
    total = order // chunk

    def copy(n):
        return pltpu.make_async_copy(matrix.at[pl.ds(n * chunk, chunk), :], buffer.at[n % 2], sems.at[n % 2])

    copy(0).start()
    for n in range(total):
        if n + 1 < total:
            copy(n + 1).start()
        copy(n).wait()
        x = buffer[n % 2]
        high, low = split(x)
        at = slice(n * chunk, (n + 1) * chunk)
        high_ref[at, :] = high
        low_ref[at, :] = low
        k, start = divmod(n * chunk, rows)
        diagonal[k, start : start + chunk, :] = buffer[n % 2, :, k * rows : (k + 1) * rows]


def inverse_kernel(mesh, roles, dirs, sizes, diagonal, *rest):
    got = rest[: len(roles)]
    high_ref, low_ref, work = rest[len(roles) :]
    rows = work.shape[-1]
    work[...] = diagonal[...]
    for n, role in enumerate(roles):
        slot, there = role_slot(mesh, dirs, role)
        work[slot] = work[slot] + jnp.where(there, 1.0, 0.0) * got[n][:, :rows]
    r = lax.broadcasted_iota(jnp.int32, (rows, rows), 0)
    c = lax.broadcasted_iota(jnp.int32, (rows, rows), 1)
    for k in range(SLOTS):
        used = jnp.maximum(r, c) < sizes[k]
        work[k] = jnp.where(used, work[k], jnp.where(r == c, 1.0, 0.0))
    invert_blocks(work)
    for k in range(SLOTS):
        high_ref[k], low_ref[k] = split(work[k])


def step_kernel(mesh, roles, first, dirs, sizes, s_high, s_low, i_high, i_low, loads, *rest):
    got, rest = rest[: len(roles)], rest[len(roles) :]
    if first:
        before = None
    else:
        (before, previous), rest = rest[:2], rest[2:]
    disp, part, rest = rest[0], rest[1], rest[2:]
    outs, (resid, pair) = rest[: len(roles)], rest[len(roles) :]
    rows, cases = i_high.shape[1], loads.shape[1]
    for k in range(SLOTS):
        at = slice(k * rows, (k + 1) * rows)
        if first:
            resid[at, :] = jnp.where(row_mask(rows, sizes[k], cases), loads[at, :], 0.0)
        else:
            resid[at, :] = previous[at, :]
    slots = [role_slot(mesh, dirs, role) for role in roles]
    for n, (slot, there) in enumerate(slots):
        at = slot_rows(slot, rows)
        here = got[n][:, got[n].shape[1] - cases :]
        resid[at, :] = resid[at, :] + jnp.where(there, 1.0, 0.0) * here
    for k in range(SLOTS):
        at = slice(k * rows, (k + 1) * rows)
        both = jnp.concatenate(split(resid[at, :]), 1)
        update = jnp.dot(i_high[k], both, preferred_element_type=F32)
        update += jnp.dot(i_low[k], both, preferred_element_type=F32)
        value = OMEGA * (update[:, :cases] + update[:, cases:])
        if before is not None:
            value = before[at, :] + value
        disp[at, :] = value
        high, low = split(value)
        pair[at, :cases] = high
        pair[at, cases:] = low
    for k in range(SLOTS):
        at = slice(k * rows, (k + 1) * rows)
        applied = jnp.dot(s_high[at, :], pair[...], preferred_element_type=F32)
        applied += jnp.dot(s_low[at, :], pair[...], preferred_element_type=F32)
        value = loads[at, :] - (applied[:, :cases] + applied[:, cases:])
        part[at, :] = jnp.where(row_mask(rows, sizes[k], cases), value, 0.0)
    for n, (slot, there) in enumerate(slots):
        outs[n][...] = part[slot_rows(slot, rows), :]


def final_kernel(mesh, roles, dirs, part, *rest):
    got, out = rest[: len(roles)], rest[len(roles)]
    rows = got[0].shape[0]
    out[...] = part[...]
    for n, role in enumerate(roles):
        slot, there = role_slot(mesh, dirs, role)
        at = slot_rows(slot, rows)
        out[at, :] = out[at, :] + jnp.where(there, 1.0, 0.0) * got[n][...]


def params(mib, **kw):
    return pltpu.CompilerParams(vmem_limit_bytes=mib << 20, **kw)


def shape(*dims, dtype=F32):
    return jax.ShapeDtypeStruct(dims, dtype)


def local(mesh, schur, loads, face_sizes, face_dir):
    matrix = schur[0, 0]
    load = loads[0, 0]
    sizes = face_sizes[0, 0]
    dirs = face_dir[0, 0]
    order, cases = load.shape
    rows = order // SLOTS
    roles = role_list(mesh)
    many = len(roles)

    sends = pl.pallas_call(
        functools.partial(pack_kernel, mesh, roles),
        name="pack",
        out_shape=[shape(rows, rows + cases)] * many,
        in_specs=[SMEM, SMEM, HBM, HBM],
        out_specs=[VMEM] * many,
        scratch_shapes=[pltpu.VMEM((many, rows, rows), F32), pltpu.VMEM((many, rows, cases), F32), pltpu.SemaphoreType.DMA((many, 2))],
        compiler_params=params(8),
    )(dirs, sizes, matrix, load)
    got = [exchange(mesh, role, value) for role, value in zip(roles, sends)]

    chunk = rows // 2
    s_high, s_low, diagonal = pl.pallas_call(
        split_kernel,
        name="split",
        out_shape=[shape(order, order, dtype=BF16), shape(order, order, dtype=BF16), shape(SLOTS, rows, rows)],
        in_specs=[HBM],
        out_specs=[VMEM] * 3,
        scratch_shapes=[pltpu.VMEM((2, chunk, order), F32), pltpu.SemaphoreType.DMA((2,))],
        compiler_params=params(20),
        cost_estimate=pl.CostEstimate(flops=4 * order * order, bytes_accessed=4 * order * order, transcendentals=0),
    )(matrix)

    i_high, i_low = pl.pallas_call(
        functools.partial(inverse_kernel, mesh, roles),
        name="inverse",
        out_shape=[shape(SLOTS, rows, rows, dtype=BF16)] * 2,
        in_specs=[SMEM, SMEM, VMEM] + [VMEM] * many,
        out_specs=[VMEM] * 2,
        scratch_shapes=[pltpu.VMEM((SLOTS, rows, rows), F32)],
        compiler_params=params(16),
    )(dirs, sizes, diagonal, *got)

    disp = part = None
    for step in range(ITERS):
        first = step == 0
        args = [dirs, sizes, s_high, s_low, i_high, i_low, load, *got] + ([] if first else [disp, part])
        disp, part, *sends = pl.pallas_call(
            functools.partial(step_kernel, mesh, roles, first),
            name=f"step{step}",
            out_shape=[shape(order, cases)] * 2 + [shape(rows, cases)] * many,
            in_specs=[SMEM, SMEM] + [VMEM] * (len(args) - 2),
            out_specs=[VMEM] * (2 + many),
            scratch_shapes=[pltpu.VMEM((order, cases), F32), pltpu.VMEM((order, 2 * cases), BF16)],
            compiler_params=params(24),
        )(*args)
        got = [exchange(mesh, role, value) for role, value in zip(roles, sends)]

    final = pl.pallas_call(
        functools.partial(final_kernel, mesh, roles),
        name="final",
        out_shape=shape(order, cases),
        in_specs=[SMEM] + [VMEM] * (1 + many),
        out_specs=VMEM,
        compiler_params=params(8),
    )(dirs, part, *got)
    return disp[None, None], final[None, None]


def solution(mesh):
    return jax.shard_map(
        functools.partial(local, mesh),
        mesh=mesh,
        in_specs=(
            P("wide", "depth", None, None),
            P("wide", "depth", None, None),
            P("wide", "depth", None),
            P("wide", "depth", None),
        ),
        out_specs=(P("wide", "depth", None, None), P("wide", "depth", None, None)),
        check_vma=False,
    )
```

```python
import functools

import jax
import jax.numpy as jnp
from jax import lax
from jax.experimental import pallas as pl
from jax.experimental.pallas import tpu as pltpu
from jax.sharding import PartitionSpec as P

ITERS = 2
OMEGA = 0.6

SLOTS = 6
LANES = 128
OUTER = 32
MICRO = 8
F32 = jnp.float32
BF16 = jnp.bfloat16
SMEM = pl.BlockSpec(memory_space=pltpu.SMEM)
VMEM = pl.BlockSpec(memory_space=pltpu.VMEM)
HBM = pl.BlockSpec(memory_space=pltpu.HBM)


def role_list(mesh):
    return [(axis, turn) for axis in ("wide", "depth") for turn in (0, 1) if mesh.shape[axis] > 1 + turn]


def role_slot(mesh, dirs_ref, role):
    axis, turn = role
    index = lax.axis_index(axis)
    count = mesh.shape[axis]
    upper = (index + turn) % 2 == 0
    facing = jnp.where(upper, 1, 0) + (0 if axis == "wide" else 2)
    slot = jnp.int32(0)
    for k in range(SLOTS):
        slot = slot + jnp.where(dirs_ref[k] == facing, k, 0)
    there = jnp.where(upper, index + 1 < count, index > 0)
    return slot, there


def exchange(mesh, role, value):
    axis, turn = role
    other = "depth" if axis == "wide" else "wide"
    count, rest = mesh.shape[axis], mesh.shape[other]
    pairs, left = [], []
    for line in range(rest):
        met = set()
        for low in range(turn, count - 1, 2):
            pairs.append(((low, line), (low + 1, line)))
            met |= {low, low + 1}
        left.append([(i, line) for i in range(count) if i not in met])
    alone = [spot for spots in left for spot in spots]
    pairs += list(zip(alone[::2], alone[1::2]))

    def flat(spot):
        place = {axis: spot[0], other: spot[1]}
        return place["wide"] * mesh.shape["depth"] + place["depth"]

    perm = []
    for one, two in pairs:
        perm += [(flat(one), flat(two)), (flat(two), flat(one))]
    return lax.ppermute(value, ("wide", "depth"), sorted(perm))


def spread_row(x, k):
    return jnp.broadcast_to(x[k : k + 1, :], x.shape)


def tree_sum(terms):
    while len(terms) > 1:
        terms = [terms[i] + terms[i + 1] if i + 1 < len(terms) else terms[i] for i in range(0, len(terms), 2)]
    return terms[0]


def invert_diagonal(d):
    rows, packs = len(d), len(d[0])
    lane = lax.broadcasted_iota(jnp.int32, (MICRO, LANES), 1)
    sub = lax.broadcasted_iota(jnp.int32, (MICRO, LANES), 0)
    half = lane - (lane & (OUTER - 1))
    local = lane & (OUTER - 1)
    for q in range(rows):
        own = (local >= q * MICRO) & (local < (q + 1) * MICRO)
        spots = [half + (q * MICRO + j) for j in range(MICRO)]
        cols = [[jnp.take_along_axis(d[q][p], spots[j], axis=1) for j in range(MICRO)] for p in range(packs)]
        scales = [[None] * MICRO for _ in range(packs)]
        for k in range(MICRO):
            pivot_row = sub == k
            for p in range(packs):
                c = cols[p]
                scale = 1.0 / spread_row(c[k], k)
                scales[p][k] = scale
                h = jnp.where(pivot_row, 0.0, c[k]) * scale
                for j in range(MICRO):
                    if j != k:
                        c[j] = c[j] - h * spread_row(c[j], k)
                c[k] = jnp.where(pivot_row, 1.0, -h)
        for p in range(packs):
            scale = scales[p][0]
            for k in range(1, MICRO):
                scale = jnp.where(sub == k, scales[p][k], scale)
            row = jnp.where(own, jnp.where(local == sub + q * MICRO, 1.0, 0.0), d[q][p])
            row = tree_sum([cols[p][j] * spread_row(row, j) for j in range(MICRO)]) * scale
            spread = [spread_row(row, j) for j in range(MICRO)]
            for step in range(1, rows):
                i = (q + step) % rows
                x = d[i][p]
                change = tree_sum([jnp.take_along_axis(x, spots[j], axis=1) * spread[j] for j in range(MICRO)])
                d[i][p] = jnp.where(own, 0.0, x) - change
            d[q][p] = row
    return d


def split(x):
    high = x.astype(BF16)
    return high, (x - high.astype(F32)).astype(BF16)


def left(x):
    return jnp.concatenate(split(x), 1)


def right(x):
    high, low = split(x)
    return jnp.concatenate([jnp.concatenate([high, low], 1), jnp.concatenate([high, jnp.zeros_like(low)], 1)], 0)


def product(one, two):
    both = jnp.dot(one, two, preferred_element_type=F32)
    half = both.shape[1] // 2
    return both[:, :half] + both[:, half:]


def lane_group(rows):
    return lax.broadcasted_iota(jnp.int32, (rows, LANES), 1) // OUTER


def packed(a_ref, rows, cl, s, fill=0.0):
    groups = LANES // OUTER
    height = rows.stop - rows.start
    group = lane_group(height)
    out = []
    for first in range(0, a_ref.shape[0], groups):
        pack = None
        for g in range(first, min(a_ref.shape[0], first + groups)):
            to = g - first
            x = a_ref[g, rows, cl]
            if to != s:
                x = pltpu.roll(x, ((to - s) * OUTER) % LANES, 1)
            pack = x if pack is None else jnp.where(group >= to, x, pack)
        if to + 1 < groups:
            spare = jnp.zeros_like(pack)
            if fill:
                spare = jnp.where(lax.broadcasted_iota(jnp.int32, pack.shape, 1) % OUTER == lax.broadcasted_iota(jnp.int32, pack.shape, 0), fill, spare)
            pack = jnp.where(group > to, spare, pack)
        out.append(pack)
    return out


def block_diagonal(x):
    group = lane_group(OUTER)
    return jnp.concatenate([jnp.where(group == k, x, 0.0) for k in range(LANES // OUTER)], 0)


def invert_tile(a_ref, rl, cl):
    count = a_ref.shape[0]
    groups = LANES // OUTER
    pieces = OUTER // MICRO
    bands = [slice(rl.start + s * OUTER, rl.start + (s + 1) * OUTER) for s in range(groups)]
    group_row, group_all = lane_group(OUTER), lane_group(LANES)
    d = packed(a_ref, bands[0], cl, 0, 1.0)
    for s in range(groups):
        lines = [[x[i * MICRO : (i + 1) * MICRO] for x in d] for i in range(pieces)]
        lines = invert_diagonal(lines)
        packs = [jnp.concatenate([lines[i][p] for i in range(pieces)], 0) for p in range(len(d))]
        if s + 1 < groups:
            ahead = packed(a_ref, bands[s], cl, s + 1)
            below = packed(a_ref, bands[s + 1], cl, s)
            d = packed(a_ref, bands[s + 1], cl, s + 1, 1.0)
            for p, w in enumerate(packs):
                row = product(left(w), right(block_diagonal(ahead[p])))
                d[p] = d[p] - product(left(below[p]), right(block_diagonal(row)))
        for g in range(count):
            p, at = divmod(g, groups)
            w = packs[p]
            if at != s:
                w = pltpu.roll(w, ((s - at) * OUTER) % LANES, 1)
            w = jnp.where(group_row == s, w, 0.0)
            t = a_ref[g, rl, cl]
            row = jnp.where(group_row == s, w, product(left(w), right(t)))
            parts = [jnp.zeros((OUTER, LANES), F32)] * groups
            parts[s] = row
            change = product(left(t), right(jnp.concatenate(parts, 0)))
            a_ref[g, rl, cl] = jnp.where(group_all == s, 0.0, t) - change
            a_ref[g, bands[s], cl] = row


def invert_blocks(a_ref):
    count, size = a_ref.shape[0], a_ref.shape[-1]
    tiles = [slice(b * LANES, (b + 1) * LANES) for b in range(size // LANES)]
    for own in tiles:
        invert_tile(a_ref, own, own)
        others = [t for t in tiles if t is not own]
        for g in range(count):
            x = a_ref[g, own, own]
            x_left, x_right = left(x), right(x)
            columns = [left(a_ref[g, t, own]) for t in others]
            rows = []
            for t in others:
                row = product(x_left, right(a_ref[g, own, t]))
                a_ref[g, own, t] = row
                rows.append(right(row))
            for i, ti in enumerate(others):
                for j, tj in enumerate(others):
                    a_ref[g, ti, tj] = a_ref[g, ti, tj] - product(columns[i], rows[j])
                a_ref[g, ti, own] = -product(columns[i], x_right)


def slot_rows(slot, rows):
    return pl.ds(pl.multiple_of(slot * rows, rows), rows)


def row_mask(rows, size, lanes=LANES):
    return lax.broadcasted_iota(jnp.int32, (rows, lanes), 0) < size


def pack_kernel(mesh, roles, dirs, sizes, matrix, loads, *rest):
    outs, (block, load, sems) = rest[: len(roles)], rest[len(roles) :]
    rows = block.shape[1]
    cases = load.shape[2]
    copies = []
    for n, role in enumerate(roles):
        slot, _ = role_slot(mesh, dirs, role)
        at = slot_rows(slot, rows)
        one = pltpu.make_async_copy(matrix.at[at, at], block.at[n], sems.at[n, 0])
        two = pltpu.make_async_copy(loads.at[at, :], load.at[n], sems.at[n, 1])
        one.start()
        two.start()
        copies.append((one, two, slot))
    for n, (one, two, slot) in enumerate(copies):
        one.wait()
        two.wait()
        outs[n][:, :rows] = block[n]
        outs[n][:, rows:] = jnp.where(row_mask(rows, sizes[slot], cases), load[n], 0.0)


def split_kernel(matrix, high_ref, low_ref, diagonal, buffer, sems):
    order = matrix.shape[0]
    rows = diagonal.shape[1]
    chunk = buffer.shape[1]
    total = order // chunk

    def copy(n):
        return pltpu.make_async_copy(matrix.at[pl.ds(n * chunk, chunk), :], buffer.at[n % 2], sems.at[n % 2])

    copy(0).start()
    for n in range(total):
        if n + 1 < total:
            copy(n + 1).start()
        copy(n).wait()
        x = buffer[n % 2]
        high, low = split(x)
        at = slice(n * chunk, (n + 1) * chunk)
        high_ref[at, :] = high
        low_ref[at, :] = low
        k, start = divmod(n * chunk, rows)
        diagonal[k, start : start + chunk, :] = buffer[n % 2, :, k * rows : (k + 1) * rows]


def inverse_kernel(mesh, roles, dirs, sizes, diagonal, *rest):
    got = rest[: len(roles)]
    high_ref, low_ref, work = rest[len(roles) :]
    rows = work.shape[-1]
    work[...] = diagonal[...]
    for n, role in enumerate(roles):
        slot, there = role_slot(mesh, dirs, role)
        work[slot] = work[slot] + jnp.where(there, 1.0, 0.0) * got[n][:, :rows]
    r = lax.broadcasted_iota(jnp.int32, (rows, rows), 0)
    c = lax.broadcasted_iota(jnp.int32, (rows, rows), 1)
    for k in range(SLOTS):
        used = jnp.maximum(r, c) < sizes[k]
        work[k] = jnp.where(used, work[k], jnp.where(r == c, 1.0, 0.0))
    invert_blocks(work)
    for k in range(SLOTS):
        high_ref[k], low_ref[k] = split(work[k])


def step_kernel(mesh, roles, first, dirs, sizes, s_high, s_low, i_high, i_low, loads, *rest):
    got, rest = rest[: len(roles)], rest[len(roles) :]
    if first:
        before = None
    else:
        (before, previous), rest = rest[:2], rest[2:]
    disp, part, rest = rest[0], rest[1], rest[2:]
    outs, (resid, pair) = rest[: len(roles)], rest[len(roles) :]
    rows, cases = i_high.shape[1], loads.shape[1]
    for k in range(SLOTS):
        at = slice(k * rows, (k + 1) * rows)
        if first:
            resid[at, :] = jnp.where(row_mask(rows, sizes[k], cases), loads[at, :], 0.0)
        else:
            resid[at, :] = previous[at, :]
    slots = [role_slot(mesh, dirs, role) for role in roles]
    for n, (slot, there) in enumerate(slots):
        at = slot_rows(slot, rows)
        here = got[n][:, got[n].shape[1] - cases :]
        resid[at, :] = resid[at, :] + jnp.where(there, 1.0, 0.0) * here
    for k in range(SLOTS):
        at = slice(k * rows, (k + 1) * rows)
        both = jnp.concatenate(split(resid[at, :]), 1)
        update = jnp.dot(i_high[k], both, preferred_element_type=F32)
        update += jnp.dot(i_low[k], both, preferred_element_type=F32)
        value = OMEGA * (update[:, :cases] + update[:, cases:])
        if before is not None:
            value = before[at, :] + value
        disp[at, :] = value
        high, low = split(value)
        pair[at, :cases] = high
        pair[at, cases:] = low
    for k in range(SLOTS):
        at = slice(k * rows, (k + 1) * rows)
        applied = jnp.dot(s_high[at, :], pair[...], preferred_element_type=F32)
        applied += jnp.dot(s_low[at, :], pair[...], preferred_element_type=F32)
        value = loads[at, :] - (applied[:, :cases] + applied[:, cases:])
        part[at, :] = jnp.where(row_mask(rows, sizes[k], cases), value, 0.0)
    for n, (slot, there) in enumerate(slots):
        outs[n][...] = part[slot_rows(slot, rows), :]


def final_kernel(mesh, roles, dirs, part, *rest):
    got, out = rest[: len(roles)], rest[len(roles)]
    rows = got[0].shape[0]
    out[...] = part[...]
    for n, role in enumerate(roles):
        slot, there = role_slot(mesh, dirs, role)
        at = slot_rows(slot, rows)
        out[at, :] = out[at, :] + jnp.where(there, 1.0, 0.0) * got[n][...]


def params(mib, **kw):
    return pltpu.CompilerParams(vmem_limit_bytes=mib << 20, **kw)


def shape(*dims, dtype=F32):
    return jax.ShapeDtypeStruct(dims, dtype)


def local(mesh, schur, loads, face_sizes, face_dir):
    matrix = schur[0, 0]
    load = loads[0, 0]
    sizes = face_sizes[0, 0]
    dirs = face_dir[0, 0]
    order, cases = load.shape
    rows = order // SLOTS
    roles = role_list(mesh)
    many = len(roles)

    sends = pl.pallas_call(
        functools.partial(pack_kernel, mesh, roles),
        name="pack",
        out_shape=[shape(rows, rows + cases)] * many,
        in_specs=[SMEM, SMEM, HBM, HBM],
        out_specs=[VMEM] * many,
        scratch_shapes=[pltpu.VMEM((many, rows, rows), F32), pltpu.VMEM((many, rows, cases), F32), pltpu.SemaphoreType.DMA((many, 2))],
        compiler_params=params(60),
    )(dirs, sizes, matrix, load)
    got = [exchange(mesh, role, value) for role, value in zip(roles, sends)]

    chunk = rows // 2
    s_high, s_low, diagonal = pl.pallas_call(
        split_kernel,
        name="split",
        out_shape=[shape(order, order, dtype=BF16), shape(order, order, dtype=BF16), shape(SLOTS, rows, rows)],
        in_specs=[HBM],
        out_specs=[VMEM] * 3,
        scratch_shapes=[pltpu.VMEM((2, chunk, order), F32), pltpu.SemaphoreType.DMA((2,))],
        compiler_params=params(40),
        cost_estimate=pl.CostEstimate(flops=4 * order * order, bytes_accessed=4 * order * order, transcendentals=0),
    )(matrix)

    i_high, i_low = pl.pallas_call(
        functools.partial(inverse_kernel, mesh, roles),
        name="inverse",
        out_shape=[shape(SLOTS, rows, rows, dtype=BF16)] * 2,
        in_specs=[SMEM, SMEM, VMEM] + [VMEM] * many,
        out_specs=[VMEM] * 2,
        scratch_shapes=[pltpu.VMEM((SLOTS, rows, rows), F32)],
        compiler_params=params(16),
    )(dirs, sizes, diagonal, *got)

    disp = part = None
    for step in range(ITERS):
        first = step == 0
        args = [dirs, sizes, s_high, s_low, i_high, i_low, load, *got] + ([] if first else [disp, part])
        disp, part, *sends = pl.pallas_call(
            functools.partial(step_kernel, mesh, roles, first),
            name=f"step{step}",
            out_shape=[shape(order, cases)] * 2 + [shape(rows, cases)] * many,
            in_specs=[SMEM, SMEM] + [VMEM] * (len(args) - 2),
            out_specs=[VMEM] * (2 + many),
            scratch_shapes=[pltpu.VMEM((order, cases), F32), pltpu.VMEM((order, 2 * cases), BF16)],
            compiler_params=params(24),
        )(*args)
        got = [exchange(mesh, role, value) for role, value in zip(roles, sends)]

    final = pl.pallas_call(
        functools.partial(final_kernel, mesh, roles),
        name="final",
        out_shape=shape(order, cases),
        in_specs=[SMEM] + [VMEM] * (1 + many),
        out_specs=VMEM,
        compiler_params=params(8),
    )(dirs, part, *got)
    return disp[None, None], final[None, None]


def solution(mesh):
    return jax.shard_map(
        functools.partial(local, mesh),
        mesh=mesh,
        in_specs=(
            P("wide", "depth", None, None),
            P("wide", "depth", None, None),
            P("wide", "depth", None),
            P("wide", "depth", None),
        ),
        out_specs=(P("wide", "depth", None, None), P("wide", "depth", None, None)),
        check_vma=False,
    )
```

```python
import functools

import jax
import jax.numpy as jnp
from jax import lax
from jax.experimental import pallas as pl
from jax.experimental.pallas import tpu as pltpu
from jax.sharding import PartitionSpec as P

ITERS = 2
OMEGA = 0.6

SLOTS = 6
LANES = 128
OUTER = 32
MICRO = 8
F32 = jnp.float32
BF16 = jnp.bfloat16
SMEM = pl.BlockSpec(memory_space=pltpu.SMEM)
VMEM = pl.BlockSpec(memory_space=pltpu.VMEM)
HBM = pl.BlockSpec(memory_space=pltpu.HBM)


def face_list(mesh):
    met, alone = [], []
    for axis, turn in (("wide", 1), ("depth", 0), ("depth", 1), ("wide", 0)):
        (met if mesh.shape[axis] > 1 + turn else alone).append((axis, turn))
    return met + alone + [4, 5], len(met)


def face_slot(mesh, dirs_ref, face):
    there = False
    if isinstance(face, int):
        facing = face
    else:
        axis, turn = face
        index = lax.axis_index(axis)
        upper = (index + turn) % 2 == 0
        facing = jnp.where(upper, 1, 0) + (0 if axis == "wide" else 2)
        there = jnp.where(upper, index + 1 < mesh.shape[axis], index > 0)
    slot = jnp.int32(0)
    for k in range(SLOTS):
        slot = slot + jnp.where(dirs_ref[k] == facing, k, 0)
    return slot, there


def exchange(mesh, face, value):
    axis, turn = face
    other = "depth" if axis == "wide" else "wide"
    count, lines = mesh.shape[axis], mesh.shape[other]
    low = range(turn, count - 1, 2)
    met = {i + more for i in low for more in (0, 1)}
    pairs = [((i, line), (i + 1, line)) for i in low for line in range(lines)]
    alone = [(i, line) for i in range(count) if i not in met for line in range(lines)]
    pairs += list(zip(alone[::2], alone[1::2]))

    def flat(spot):
        place = {axis: spot[0], other: spot[1]}
        return place["wide"] * mesh.shape["depth"] + place["depth"]

    perm = [(flat(a), flat(b)) for a, b in pairs]
    perm += [(b, a) for a, b in perm]
    return lax.ppermute(value, ("wide", "depth"), sorted(perm))


def spread_row(x, k):
    return jnp.broadcast_to(x[k : k + 1, :], x.shape)


def tree_sum(terms):
    while len(terms) > 1:
        terms = [terms[i] + terms[i + 1] if i + 1 < len(terms) else terms[i] for i in range(0, len(terms), 2)]
    return terms[0]


def invert_diagonal(d, fill=lambda: None):
    rows, packs = len(d), len(d[0])
    lane = lax.broadcasted_iota(jnp.int32, (MICRO, LANES), 1)
    sub = lax.broadcasted_iota(jnp.int32, (MICRO, LANES), 0)
    half = lane - (lane & (OUTER - 1))
    local = lane & (OUTER - 1)
    for q in range(rows):
        own = (local >= q * MICRO) & (local < (q + 1) * MICRO)
        spots = [half + (q * MICRO + j) for j in range(MICRO)]
        cols = [[jnp.take_along_axis(d[q][p], spots[j], axis=1) for j in range(MICRO)] for p in range(packs)]
        scales = [[None] * MICRO for _ in range(packs)]
        for k in range(MICRO):
            pivot_row = sub == k
            for p in range(packs):
                c = cols[p]
                scale = 1.0 / spread_row(c[k], k)
                scales[p][k] = scale
                h = jnp.where(pivot_row, 0.0, c[k]) * scale
                for j in range(MICRO):
                    if j != k:
                        c[j] = c[j] - h * spread_row(c[j], k)
                c[k] = jnp.where(pivot_row, 1.0, -h)
            if k % 2:
                fill()
        for p in range(packs):
            scale = scales[p][0]
            for k in range(1, MICRO):
                scale = jnp.where(sub == k, scales[p][k], scale)
            row = jnp.where(own, jnp.where(local == sub + q * MICRO, 1.0, 0.0), d[q][p])
            row = tree_sum([cols[p][j] * spread_row(row, j) for j in range(MICRO)]) * scale
            spread = [spread_row(row, j) for j in range(MICRO)]
            for step in range(1, rows):
                i = (q + step) % rows
                x = d[i][p]
                change = tree_sum([jnp.take_along_axis(x, spots[j], axis=1) * spread[j] for j in range(MICRO)])
                d[i][p] = jnp.where(own, 0.0, x) - change
            d[q][p] = row
    return d


def split(x):
    high = x.astype(BF16)
    return high, (x - high.astype(F32)).astype(BF16)


def left(x):
    return jnp.concatenate(split(x), 1)


def right(x):
    high, low = split(x)
    return jnp.concatenate([jnp.concatenate([high, low], 1), jnp.concatenate([high, jnp.zeros_like(low)], 1)], 0)


def product(one, two):
    both = jnp.dot(one, two, preferred_element_type=F32)
    half = both.shape[1] // 2
    return both[:, :half] + both[:, half:]


def lane_group(rows):
    return lax.broadcasted_iota(jnp.int32, (rows, LANES), 1) // OUTER


def packed(a_ref, rows, cl, s, fill=0.0):
    groups = LANES // OUTER
    height = rows.stop - rows.start
    group = lane_group(height)
    out = []
    for first in range(0, a_ref.shape[0], groups):
        pack = None
        for g in range(first, min(a_ref.shape[0], first + groups)):
            to = g - first
            x = a_ref[g, rows, cl]
            if to != s:
                x = pltpu.roll(x, ((to - s) * OUTER) % LANES, 1)
            pack = x if pack is None else jnp.where(group >= to, x, pack)
        if to + 1 < groups:
            spare = jnp.zeros_like(pack)
            if fill:
                spare = jnp.where(lax.broadcasted_iota(jnp.int32, pack.shape, 1) % OUTER == lax.broadcasted_iota(jnp.int32, pack.shape, 0), fill, spare)
            pack = jnp.where(group > to, spare, pack)
        out.append(pack)
    return out


def block_diagonal(x):
    group = lane_group(OUTER)
    return jnp.concatenate([jnp.where(group == k, x, 0.0) for k in range(LANES // OUTER)], 0)


def tile_update(a_ref, rl, cl, s, packs):
    groups = LANES // OUTER
    group_row, group_all = lane_group(OUTER), lane_group(LANES)
    band = slice(rl.start + s * OUTER, rl.start + (s + 1) * OUTER)
    count = a_ref.shape[0]

    def first(g):
        p, at = divmod(g, groups)
        w = packs[p]
        if at != s:
            w = pltpu.roll(w, ((s - at) * OUTER) % LANES, 1)
        w = jnp.where(group_row == s, w, 0.0)
        t = a_ref[g, rl, cl]
        return w, t, product(left(w), right(t))

    def second(g, w, t, row):
        row = jnp.where(group_row == s, w, row)
        parts = [jnp.zeros((OUTER, LANES), F32)] * groups
        parts[s] = row
        change = product(left(t), right(jnp.concatenate(parts, 0)))
        return t, row, change

    def third(g, t, row, change):
        a_ref[g, rl, cl] = jnp.where(group_all == s, 0.0, t) - change
        a_ref[g, band, cl] = row

    one, two = {}, {}
    for step in range(count + 2):
        if step < count:
            one[step] = first(step)
            yield
        if 0 <= step - 1 < count:
            two[step - 1] = second(step - 1, *one.pop(step - 1))
            yield
        if 0 <= step - 2 < count:
            third(step - 2, *two.pop(step - 2))
            yield


def invert_tile(a_ref, rl, cl):
    groups = LANES // OUTER
    pieces = OUTER // MICRO
    bands = [slice(rl.start + s * OUTER, rl.start + (s + 1) * OUTER) for s in range(groups)]
    d = packed(a_ref, bands[0], cl, 0, 1.0)
    rest = iter(())
    for s in range(groups):
        lines = [[x[i * MICRO : (i + 1) * MICRO] for x in d] for i in range(pieces)]
        lines = invert_diagonal(lines, lambda: next(rest, None))
        for _ in rest:
            pass
        packs = [jnp.concatenate([lines[i][p] for i in range(pieces)], 0) for p in range(len(d))]
        if s + 1 < groups:
            ahead = packed(a_ref, bands[s], cl, s + 1)
            below = packed(a_ref, bands[s + 1], cl, s)
            d = packed(a_ref, bands[s + 1], cl, s + 1, 1.0)
            rows = [product(left(w), right(block_diagonal(ahead[p]))) for p, w in enumerate(packs)]
            changes = [product(left(below[p]), right(block_diagonal(row))) for p, row in enumerate(rows)]
            d = [x - change for x, change in zip(d, changes)]
        rest = tile_update(a_ref, rl, cl, s, packs)
    for _ in rest:
        pass


def invert_blocks(a_ref):
    count, size = a_ref.shape[0], a_ref.shape[-1]
    tiles = [slice(b * LANES, (b + 1) * LANES) for b in range(size // LANES)]
    for own in tiles:
        invert_tile(a_ref, own, own)
        others = [t for t in tiles if t is not own]
        lefts = [left(a_ref[g, own, own]) for g in range(count)]
        rights = [right(a_ref[g, own, own]) for g in range(count)]
        columns = [[left(a_ref[g, t, own]) for t in others] for g in range(count)]
        rows = [[product(lefts[g], right(a_ref[g, own, t])) for t in others] for g in range(count)]
        for g in range(count):
            for i, ti in enumerate(others):
                a_ref[g, ti, own] = -product(columns[g][i], rights[g])
        for g in range(count):
            for j, tj in enumerate(others):
                a_ref[g, own, tj] = rows[g][j]
                row = right(rows[g][j])
                for i, ti in enumerate(others):
                    a_ref[g, ti, tj] = a_ref[g, ti, tj] - product(columns[g][i], row)


def slot_rows(slot, rows):
    return pl.ds(pl.multiple_of(slot * rows, rows), rows)


def row_mask(rows, size, lanes=LANES):
    return lax.broadcasted_iota(jnp.int32, (rows, lanes), 0) < size


def corner(size):
    row = lax.broadcasted_iota(jnp.int32, (size, size), 0)
    return row, lax.broadcasted_iota(jnp.int32, (size, size), 1)


def pack_kernel(mesh, faces, many, dirs, matrix, *rest):
    outs, (block, sems) = rest[:many], rest[many:]
    rows = block.shape[1]
    half = rows // 2
    copies = []
    for n in range(many):
        slot, _ = face_slot(mesh, dirs, faces[n])
        at = slot_rows(slot, rows)
        copies.append(pltpu.make_async_copy(matrix.at[at, at], block.at[n], sems.at[n]))
        copies[-1].start()
    row, col = corner(half)
    for n in range(many):
        copies[n].wait()
        last = block[n, half:, half:]
        outs[n][:half, :] = jnp.where(row >= col, block[n, :half, :half], last)
        outs[n][half:rows, :] = block[n, half:, :half]
        diagonal = jnp.where(row == col, last, 0.0).sum(axis=0, keepdims=True)
        outs[n][rows:, :] = jnp.broadcast_to(diagonal, (outs[n].shape[0] - rows, half))


def unpacked(packed_ref, rows):
    half = rows // 2
    row, col = corner(half)
    fold = packed_ref[:half, :]
    turned = fold.T
    low = packed_ref[half:rows, :]
    diagonal = jnp.broadcast_to(packed_ref[rows : rows + 1, :], (half, half))
    first = jnp.where(row >= col, fold, turned)
    last = jnp.where(row < col, fold, jnp.where(row > col, turned, diagonal))
    return first, low.T, low, last


def split_kernel(mesh, faces, many, dirs, matrix, loads, high_ref, low_ref, diagonal, *rest):
    outs, (buffer, sems, load_sem) = rest[:many], rest[many:]
    order = matrix.shape[0]
    rows = diagonal.shape[1]
    depth, chunk = buffer.shape[:2]
    total = order // chunk

    def copy(n):
        return pltpu.make_async_copy(matrix.at[pl.ds(n * chunk, chunk), :], buffer.at[n % depth], sems.at[n % depth])

    for n in range(min(depth, total)):
        copy(n).start()
    copies = []
    for n in range(many):
        slot, _ = face_slot(mesh, dirs, faces[n])
        copies.append(pltpu.make_async_copy(loads.at[slot_rows(slot, rows), :], outs[n], load_sem.at[n]))
        copies[-1].start()
    for n in range(total):
        copy(n).wait()
        at = slice(n * chunk, (n + 1) * chunk)
        high, low = split(buffer[n % depth])
        high_ref[at, :] = high
        low_ref[at, :] = low
        k, start = divmod(n * chunk, rows)
        diagonal[k, start : start + chunk, :] = buffer[n % depth, :, k * rows : (k + 1) * rows]
        if n + depth < total:
            copy(n + depth).start()
    for one in copies:
        one.wait()


def inverse_kernel(mesh, faces, many, dirs, sizes, diagonal, *rest):
    got, (high_ref, low_ref, work) = rest[:many], rest[many:]
    rows = work.shape[-1]
    half = rows // 2
    work[...] = diagonal[...]
    for n in range(many):
        slot, there = face_slot(mesh, dirs, faces[n])
        factor = jnp.where(there, 1.0, 0.0)
        parts = unpacked(got[n], rows)
        for k, part in enumerate(parts):
            i, j = divmod(k, 2)
            at = (slot, slice(i * half, (i + 1) * half), slice(j * half, (j + 1) * half))
            work[at] = work[at] + factor * part
    row, col = corner(rows)
    for k in range(SLOTS):
        used = jnp.maximum(row, col) < sizes[k]
        work[k] = jnp.where(used, work[k], jnp.where(row == col, 1.0, 0.0))
    invert_blocks(work)
    for k in range(SLOTS):
        high_ref[k], low_ref[k] = split(work[k])


def apply_face(slot, sizes, s_high, s_low, pair, loads, out):
    rows, cases = out.shape
    at = slot_rows(slot, rows)
    both = jnp.dot(s_high[at, :], pair[...], preferred_element_type=F32)
    both += jnp.dot(s_low[at, :], pair[...], preferred_element_type=F32)
    value = loads[at, :] - (both[:, :cases] + both[:, cases:])
    out[...] = jnp.where(row_mask(rows, sizes[slot], cases), value, 0.0)


def lead_kernel(mesh, faces, many, first, dirs, sizes, s_high, s_low, i_high, i_low, loads, *rest):
    got, rest = rest[:many], rest[many:]
    before = parts = None
    if not first:
        before, parts, rest = rest[0], rest[1 : 1 + len(faces)], rest[1 + len(faces) :]
    disp, pair, out = rest
    rows, cases = out.shape
    for n, face in enumerate(faces):
        slot, there = face_slot(mesh, dirs, face)
        at = slot_rows(slot, rows)
        if first:
            value = loads[at, :]
        else:
            value = parts[n][...]
        if n < many:
            value = value + jnp.where(there, 1.0, 0.0) * got[n][...]
        if first:
            value = jnp.where(row_mask(rows, sizes[slot], cases), value, 0.0)
        both = jnp.concatenate(split(value), 1)
        update = jnp.dot(i_high[slot], both, preferred_element_type=F32)
        update += jnp.dot(i_low[slot], both, preferred_element_type=F32)
        value = OMEGA * (update[:, :cases] + update[:, cases:])
        if before is not None:
            value = before[at, :] + value
        disp[at, :] = value
        pair[at, :cases], pair[at, cases:] = split(value)
    slot, _ = face_slot(mesh, dirs, faces[0])
    apply_face(slot, sizes, s_high, s_low, pair, loads, out)


def more_kernel(mesh, some, dirs, sizes, s_high, s_low, pair, loads, *outs):
    for face, out in zip(some, outs):
        slot, _ = face_slot(mesh, dirs, face)
        apply_face(slot, sizes, s_high, s_low, pair, loads, out)


def final_kernel(mesh, faces, many, dirs, *rest):
    parts, got, out = rest[: len(faces)], rest[len(faces) : len(faces) + many], rest[-1]
    rows = parts[0].shape[0]
    for n, face in enumerate(faces):
        slot, there = face_slot(mesh, dirs, face)
        value = parts[n][...]
        if n < many:
            value = value + jnp.where(there, 1.0, 0.0) * got[n][...]
        out[slot_rows(slot, rows), :] = value


def params(mib, **kw):
    return pltpu.CompilerParams(vmem_limit_bytes=mib << 20, **kw)


def shape(*dims, dtype=F32):
    return jax.ShapeDtypeStruct(dims, dtype)


def cost(flops, touched=0):
    return pl.CostEstimate(flops=flops, bytes_accessed=touched, transcendentals=0)


def local(mesh, schur, loads, face_sizes, face_dir):
    matrix = schur[0, 0]
    load = loads[0, 0]
    sizes = face_sizes[0, 0]
    dirs = face_dir[0, 0]
    order, cases = load.shape
    rows = order // SLOTS
    faces, many = face_list(mesh)

    def swap(sends):
        return [exchange(mesh, face, value) for face, value in zip(faces[:many], sends)]

    blocks = pl.pallas_call(
        functools.partial(pack_kernel, mesh, faces, many),
        name="pack",
        out_shape=[shape(rows + 8, rows // 2)] * many,
        in_specs=[SMEM, HBM],
        out_specs=[VMEM] * many,
        scratch_shapes=[pltpu.VMEM((many, rows, rows), F32), pltpu.SemaphoreType.DMA((many,))],
        compiler_params=params(56),
    )(dirs, matrix)
    blocks = swap(blocks)

    chunk, ahead = rows // 2, 6
    s_high, s_low, diagonal, *sends = pl.pallas_call(
        functools.partial(split_kernel, mesh, faces, many),
        name="split",
        out_shape=[shape(order, order, dtype=BF16)] * 2 + [shape(SLOTS, rows, rows)] + [shape(rows, cases)] * many,
        in_specs=[SMEM, HBM, HBM],
        out_specs=[VMEM] * (3 + many),
        scratch_shapes=[pltpu.VMEM((ahead, chunk, order), F32), pltpu.SemaphoreType.DMA((ahead,)), pltpu.SemaphoreType.DMA((many,))],
        compiler_params=params(40),
        cost_estimate=cost(4 * order * order, 4 * order * order),
    )(dirs, matrix, load)
    got = swap(sends)

    i_high, i_low = pl.pallas_call(
        functools.partial(inverse_kernel, mesh, faces, many),
        name="inverse",
        out_shape=[shape(SLOTS, rows, rows, dtype=BF16)] * 2,
        in_specs=[SMEM, SMEM, VMEM] + [VMEM] * many,
        out_specs=[VMEM] * 2,
        scratch_shapes=[pltpu.VMEM((SLOTS, rows, rows), F32)],
        compiler_params=params(16),
        cost_estimate=cost(2 * SLOTS * rows**3 * 40),
    )(dirs, sizes, diagonal, *blocks)

    disp = parts = None
    for step in range(ITERS):
        first = step == 0
        args = [dirs, sizes, s_high, s_low, i_high, i_low, load, *got] + ([] if first else [disp, *parts])
        disp, pair, part = pl.pallas_call(
            functools.partial(lead_kernel, mesh, faces, many, first),
            name=f"lead{step}",
            out_shape=[shape(order, cases), shape(order, 2 * cases, dtype=BF16), shape(rows, cases)],
            in_specs=[SMEM, SMEM] + [VMEM] * (len(args) - 2),
            out_specs=[VMEM] * 3,
            compiler_params=params(16),
            cost_estimate=cost(6 * rows * order * cases),
        )(*args)
        parts = [part]
        while len(parts) < SLOTS:
            at = len(parts)
            some = faces[at : at + 1] if at < many else faces[at:]
            parts += pl.pallas_call(
                functools.partial(more_kernel, mesh, some),
                name=f"more{step}",
                out_shape=[shape(rows, cases)] * len(some),
                in_specs=[SMEM, SMEM] + [VMEM] * 4,
                out_specs=[VMEM] * len(some),
                compiler_params=params(16),
                cost_estimate=cost(6 * rows * order * cases * len(some)),
            )(dirs, sizes, s_high, s_low, pair, load)
        got = swap(parts)

    final = pl.pallas_call(
        functools.partial(final_kernel, mesh, faces, many),
        name="final",
        out_shape=shape(order, cases),
        in_specs=[SMEM] + [VMEM] * (SLOTS + many),
        out_specs=VMEM,
        compiler_params=params(8),
    )(dirs, *parts, *got)
    return disp[None, None], final[None, None]


def solution(mesh):
    return jax.shard_map(
        functools.partial(local, mesh),
        mesh=mesh,
        in_specs=(
            P("wide", "depth", None, None),
            P("wide", "depth", None, None),
            P("wide", "depth", None),
            P("wide", "depth", None),
        ),
        out_specs=(P("wide", "depth", None, None), P("wide", "depth", None, None)),
        check_vma=False,
    )
```
